256 devices in a mesh: grp: 32 (over x, y, core), dom: 8 (over z).
Axes of the slice: x: 4, y: 4, z: 8, core: 2. Of those that a mesh axis runs over, the one named last changes fastest.
Arguments:
- surplus: float32 [512, 1024, 512], P('grp', 'dom'), may hold values from -0.4 to 0.4
- block_ids: int32 [512, 1024], P('grp', 'dom'), may hold values from 0 to 8191, as said below
- coef: int32 [512], P('grp'), may hold values from -4 to 6, as said below
Outputs:
- updated: float32 [512, 1024, 512], P('grp', 'dom')
The draws below stay inside these ranges and needn't reach their ends.
Inputs may be any that keep to these rules, and one draw needn't show every extreme that they name: `block_ids`: for each grid, the slots in columns d * 128 to (d + 1) * 128 - 1 hold 128 different numbers from d * 1024 to (d + 1) * 1024 - 1. `coef`: each coefficient is one of 1, -4, 6.
All inputs are finite; a program needn't handle non-finite values.
Results may differ from the reference program's by a relative error of at most 0.000071.
Values sent between devices are 32-bit elements; how exact they have to be, the bound alone decides.
No kernel may reach another device: no remote copies, remote signals or barrier semaphores. Data moves between devices by JAX's collectives and lax.ppermute only.
A program may use at most 64 MiB of HBM per device.

```python
import jax
import jax.numpy as jnp

K = 128
NBD = 1024
BLK = 512
GRIDS = 512
BLOCKS = 8192
N_DOM = 8


def draw_block_ids(key, part):
    keys = jax.random.split(jax.random.fold_in(key, 11), GRIDS * N_DOM)
    picked = jax.vmap(lambda single: jax.random.permutation(single, NBD)[:K])(keys)
    picked = picked.reshape(GRIDS, N_DOM, K).astype(jnp.int32)
    offsets = (jnp.arange(N_DOM, dtype=jnp.int32) * NBD)[None, :, None]
    return (picked + offsets).reshape(GRIDS, N_DOM * K)


def draw_coef(key, part):
    picks = jax.random.randint(jax.random.fold_in(key, 23), (GRIDS,), 0, 5)
    table = jnp.array([1, -4, 6, -4, 1], jnp.int32)
    return table[picks]


def steps_of(own_key, shape, shards, least, top_value):
    factor_of, own = 1.0, jax.random.fold_in(own_key, 6)
    for position, parts in shards:
        steps = jnp.exp(jax.random.uniform(jax.random.fold_in(own, position), (parts,), jnp.float32, least / len(shards), top_value / len(shards)))
        factor_of = factor_of * jnp.repeat(steps, shape[position] // parts).reshape([-1 if axis == position else 1 for axis in range(len(shape))])
    return factor_of


def normal_values(rng, dims, width, bound, shards=(), held_as=jnp.bfloat16):
    loudness = steps_of(rng, dims, shards, -0.22, 0.18) if shards else 1.0
    result = jax.random.normal(rng, dims, jnp.float32) * width * loudness
    return jnp.minimum(jnp.maximum(result, -bound), bound).astype(held_as)


def setup_inputs(seed: int = 0) -> dict:
    splits = jax.random.split(jax.random.key(seed), 4)
    return {
        "surplus": normal_values(splits[0], (GRIDS, N_DOM * K, BLK), 0.05, 0.4, ((0, 32), (1, 8)), jnp.float32),
        "block_ids": draw_block_ids(jax.random.fold_in(splits[3], 71), 0),
        "coef": draw_coef(jax.random.fold_in(splits[3], 71), 0),
    }


def reference(surplus, block_ids, coef):
    scaled = surplus * coef.astype(jnp.float32)[:, None, None]
    flat_ids = block_ids.reshape(-1).astype(jnp.int32)
    combined = jnp.zeros((BLOCKS, BLK), jnp.float32)
    combined = combined.at[flat_ids].add(scaled.reshape(-1, BLK))
    return combined[block_ids]
```

```python
import jax
import jax.numpy as jnp
from jax import lax
from jax.experimental import pallas as pl
from jax.experimental.pallas import tpu as pltpu
from jax.sharding import PartitionSpec as P

GRIDS = 16
K = 128
BLK = 512
NBD = 1024
HALF = NBD // 2
ROWS = HALF // 4
CHUNK = 4
VMEM = pltpu.VMEM
VMEM_LIMIT = 48 * 1024 * 1024


def device(x, y, core):
    return (x * 4 + y) * 2 + core


def pairs(partner):
    return [
        (device(x, y, c), device(*partner(x, y, c)))
        for x in range(4)
        for y in range(4)
        for c in range(2)
    ]


def own_line(step):
    return pairs(lambda x, y, c: (x, y ^ step, c) if c else (x ^ step, y, c))


def other_line(step):
    return pairs(lambda x, y, c: (x ^ step, y, c) if c else (x, y ^ step, c))


OTHER_CORE = pairs(lambda x, y, c: (x, y, 1 - c))


def send(value, partner):
    return lax.ppermute(value, "grp", partner)


def split(value):
    high = value.astype(jnp.bfloat16)
    low = (value - high.astype(jnp.float32)).astype(jnp.bfloat16)
    return high, low


def weights(ids_ref, coef_ref, where_ref, half, rows, grids):
    base = where_ref[0] + half * HALF
    line = where_ref[1 + half]
    block = lax.broadcasted_iota(jnp.int32, (ROWS, K), 0)
    columns = []
    for g in grids:
        slot = ids_ref[pl.ds(g, 1), :] - base
        quarters = []
        for k in range(4):
            hit = block == slot - (line ^ k) * ROWS
            quarters.append(jnp.where(hit, coef_ref[g].astype(jnp.float32), 0.0))
        columns.append(jnp.concatenate(quarters, 0).astype(jnp.bfloat16))
    return jnp.concatenate(columns, 1)


def scatter_other(where_ref, coef_ref, ids_ref, surplus_ref, out_ref, high_ref, low_ref, stage, sems):
    copies = []
    for t in range(GRIDS // CHUNK):
        part = pl.ds(t * CHUNK * K, CHUNK * K)
        copy = pltpu.make_async_copy(surplus_ref.at[part, :], stage.at[part, :], sems.at[t])
        copy.start()
        copies.append(copy)
    half = 1 - where_ref[3]
    for t in range(GRIDS // CHUNK):
        part = pl.ds(t * CHUNK * K, CHUNK * K)
        hot = weights(ids_ref, coef_ref, where_ref, half, ROWS, range(t * CHUNK, (t + 1) * CHUNK))
        copies[t].wait()
        high, low = split(stage[part, :])
        high_ref[part, :] = high
        low_ref[part, :] = low
        term = jnp.dot(hot, high, preferred_element_type=jnp.float32) + jnp.dot(
            hot, low, preferred_element_type=jnp.float32
        )
        if t == 0:
            out_ref[...] = term
        else:
            out_ref[...] += term


def scatter_own(where_ref, coef_ref, ids_ref, high_ref, low_ref, out_ref):
    half = where_ref[3]
    for t in range(GRIDS // CHUNK):
        part = pl.ds(t * CHUNK * K, CHUNK * K)
        hot = weights(ids_ref, coef_ref, where_ref, half, ROWS, range(t * CHUNK, (t + 1) * CHUNK))
        term = jnp.dot(hot, high_ref[part, :], preferred_element_type=jnp.float32) + jnp.dot(
            hot, low_ref[part, :], preferred_element_type=jnp.float32
        )
        if t == 0:
            out_ref[...] = term
        else:
            out_ref[...] += term


def gather(where_ref, ids_ref, *refs):
    pieces, (out_ref, high_ref, low_ref, column_ref) = refs[:8], refs[8:]
    step = pl.program_id(0)

    @pl.when(step == 0)
    def _():
        for side in range(2):
            half = where_ref[3] if side == 0 else 1 - where_ref[3]
            line = where_ref[1 + half]
            for k in range(4):
                rows = pl.ds(pl.multiple_of(half * HALF + (line ^ k) * ROWS, ROWS), ROWS)
                high, low = split(pieces[side * 4 + k][...])
                high_ref[rows, :] = high
                low_ref[rows, :] = low
        column_ref[...] = jnp.transpose(jnp.concatenate([ids_ref[...] - where_ref[0]] * 8, 0))

    block = lax.broadcasted_iota(jnp.int32, (K, NBD), 1)
    lane = lax.broadcasted_iota(jnp.int32, (K, K), 1)
    hots = []
    for i in range(CHUNK):
        column = jnp.sum(jnp.where(lane == step * CHUNK + i, column_ref[...], 0), 1, keepdims=True)
        hots.append(jnp.where(block == column, 1.0, 0.0).astype(jnp.bfloat16))
    hot = jnp.concatenate(hots, 0)
    out_ref[...] = jnp.dot(hot, high_ref[...], preferred_element_type=jnp.float32) + jnp.dot(
        hot, low_ref[...], preferred_element_type=jnp.float32
    )


def local(surplus, block_ids, coef):
    index = lax.axis_index("grp")
    core, x, y = index & 1, index >> 3, (index >> 1) & 3
    where = jnp.stack([lax.axis_index("dom") * NBD, x, y, core]).astype(jnp.int32)
    smem = pl.BlockSpec(memory_space=pltpu.SMEM)
    vmem = pl.BlockSpec(memory_space=VMEM)
    params = pltpu.CompilerParams(vmem_limit_bytes=VMEM_LIMIT)
    slots = GRIDS * K
    other, high, low = pl.pallas_call(
        scatter_other,
        out_shape=(
            jax.ShapeDtypeStruct((HALF, BLK), jnp.float32),
            jax.ShapeDtypeStruct((slots, BLK), jnp.bfloat16),
            jax.ShapeDtypeStruct((slots, BLK), jnp.bfloat16),
        ),
        in_specs=[smem, smem, vmem, pl.BlockSpec(memory_space=pl.ANY)],
        out_specs=(vmem, vmem, vmem),
        scratch_shapes=[VMEM((slots, BLK), jnp.float32), pltpu.SemaphoreType.DMA((GRIDS // CHUNK,))],
        compiler_params=params,
    )(where, coef, block_ids, surplus.reshape(slots, BLK))
    arrived = send(other, OTHER_CORE)
    own = pl.pallas_call(
        scatter_own,
        out_shape=jax.ShapeDtypeStruct((HALF, BLK), jnp.float32),
        in_specs=[smem, smem, vmem, vmem, vmem],
        out_specs=vmem,
        compiler_params=params,
        cost_estimate=pl.CostEstimate(flops=4 * HALF * slots * BLK, bytes_accessed=0, transcendentals=0),
    )(where, coef, block_ids, high, low)
    parts = [own[k * ROWS : (k + 1) * ROWS] + arrived[k * ROWS : (k + 1) * ROWS] for k in range(4)]
    order = (2, 1, 3)
    got = [send(parts[k], own_line(k)) for k in order]
    share = parts[0] + got[0] + got[1] + got[2]
    got = [send(share, other_line(k)) for k in order]
    share = share + got[0] + got[1] + got[2]
    line = [share] + [send(share, own_line(k)) for k in (1, 2, 3)]
    across = [send(piece, OTHER_CORE) for piece in line]
    out = pl.pallas_call(
        gather,
        grid=(GRIDS // CHUNK,),
        out_shape=jax.ShapeDtypeStruct((slots, BLK), jnp.float32),
        in_specs=[smem, vmem] + [vmem] * 8,
        out_specs=pl.BlockSpec((CHUNK * K, BLK), lambda t: (t, 0)),
        scratch_shapes=[
            VMEM((NBD, BLK), jnp.bfloat16),
            VMEM((NBD, BLK), jnp.bfloat16),
            VMEM((K, K), jnp.int32),
        ],
        compiler_params=params,
    )(where, block_ids, *line, *across)
    return out.reshape(surplus.shape)


def solution(mesh):
    return jax.shard_map(
        local,
        mesh=mesh,
        in_specs=(P("grp", "dom", None), P("grp", "dom"), P("grp")),
        out_specs=P("grp", "dom", None),
        check_vma=False,
    )
```

```python
import jax
import jax.numpy as jnp
from jax import lax
from jax.experimental import pallas as pl
from jax.experimental.pallas import tpu as pltpu
from jax.sharding import PartitionSpec as P

GRIDS = 16
K = 128
BLK = 512
NBD = 1024
LANES = 128
SUB = BLK // LANES
GRID_ROWS = K * SUB
HALF = NBD // 2 * SUB
PIECE = HALF // 4
BATCH = 16
PAD = 64
VMEM = pltpu.VMEM
VMEM_LIMIT = 48 * 1024 * 1024


def device(x, y, core):
    return (x * 4 + y) * 2 + core


def pairs(partner):
    return [
        (device(x, y, c), device(*partner(x, y, c)))
        for x in range(4)
        for y in range(4)
        for c in range(2)
    ]


def own_line(step):
    return pairs(lambda x, y, c: (x, y ^ step, c) if c else (x ^ step, y, c))


def other_line(step):
    return pairs(lambda x, y, c: (x ^ step, y, c) if c else (x, y ^ step, c))


OTHER_CORE = pairs(lambda x, y, c: (x, y, 1 - c))


def send(value, partner):
    return lax.ppermute(value, "grp", partner)


def to_tiles(value):
    g, slots, _ = value.shape
    return value.reshape(g, slots // 8, 8, SUB, LANES).transpose(0, 1, 3, 2, 4).reshape(-1, LANES)


def from_tiles(rows, shape):
    g, slots, blk = shape
    return rows.reshape(g, slots // 8, SUB, 8, LANES).transpose(0, 1, 3, 2, 4).reshape(shape)


def slot_rows(start, slot):
    return pl.ds(start + (slot // 8) * 8 * SUB + slot % 8, SUB, stride=8)


def block_rows(row):
    return pl.ds(pl.multiple_of(row, SUB), SUB)


def piece_rows(where_ref, half, k):
    line = where_ref[1 + half]
    return pl.ds(pl.multiple_of(half * HALF + (line ^ k) * PIECE, PIECE), PIECE)


def scatter(where_ref, coef_hbm, ids_hbm, surplus_hbm, *refs):
    pieces, (table, stage, ids, coef, sems, small_sems) = refs[:8], refs[8:]

    def load(g):
        part = pl.ds(pl.multiple_of(g * GRID_ROWS, GRID_ROWS), GRID_ROWS)
        return pltpu.make_async_copy(surplus_hbm.at[part, :], stage.at[part, :], sems.at[g])

    ids_copy = pltpu.make_async_copy(ids_hbm, ids, small_sems.at[0])
    coef_copy = pltpu.make_async_copy(coef_hbm, coef, small_sems.at[1])
    ids_copy.start()
    coef_copy.start()
    for g in range(GRIDS):
        load(g).start()
    table[...] = jnp.zeros_like(table)
    base = where_ref[0]
    ids_copy.wait()
    coef_copy.wait()

    def add_grid(g, carry):
        load(g).wait()
        factor = coef[g].astype(jnp.float32)
        start = pl.multiple_of(g * GRID_ROWS, GRID_ROWS)
        for first in range(0, K, BATCH):
            slots = range(first, first + BATCH)
            rows = [block_rows((ids[g, j] - base) * SUB) for j in slots]
            sums = [table[r, :] + stage[slot_rows(start, j), :] * factor for r, j in zip(rows, slots)]
            for r, total in zip(rows, sums):
                table[r, :] = total
        return carry

    lax.fori_loop(0, GRIDS, add_grid, 0)
    core = where_ref[3]
    for k in range(4):
        pieces[k][...] = table[piece_rows(where_ref, 1 - core, k), :]
        pieces[4 + k][...] = table[piece_rows(where_ref, core, k), :]


def gather(where_ref, rows_vmem, *refs):
    pieces, (out_hbm, table, stage, rows_ref, sems, rows_sem) = refs[:8], refs[8:]
    rows_copy = pltpu.make_async_copy(rows_vmem, rows_ref, rows_sem)
    rows_copy.start()
    core = where_ref[3]
    for k in range(4):
        table[piece_rows(where_ref, core, k), :] = pieces[k][...]
        table[piece_rows(where_ref, 1 - core, k), :] = pieces[4 + k][...]
    rows_copy.wait()

    def store(g):
        part = pl.ds(pl.multiple_of(g * GRID_ROWS, GRID_ROWS), GRID_ROWS)
        return pltpu.make_async_copy(stage.at[part, :], out_hbm.at[part, :], sems.at[g])

    def copy_grid(g, carry):
        start = pl.multiple_of(g * GRID_ROWS, GRID_ROWS)
        for first in range(0, K, BATCH):
            slots = range(first, first + BATCH)
            values = [table[block_rows(rows_ref[g, j]), :] for j in slots]
            for j, value in zip(slots, values):
                stage[slot_rows(start, j), :] = value
        store(g).start()
        return carry

    lax.fori_loop(0, GRIDS, copy_grid, 0)
    for g in range(GRIDS):
        store(g).wait()


def local(surplus, block_ids, coef):
    index = lax.axis_index("grp")
    base = lax.axis_index("dom") * NBD
    where = jnp.stack([base, index >> 3, (index >> 1) & 3, index & 1]).astype(jnp.int32)
    smem = pl.BlockSpec(memory_space=pltpu.SMEM)
    vmem = pl.BlockSpec(memory_space=VMEM)
    hbm = pl.BlockSpec(memory_space=pltpu.HBM)
    params = pltpu.CompilerParams(vmem_limit_bytes=VMEM_LIMIT)
    piece = jax.ShapeDtypeStruct((PIECE, LANES), jnp.float32)
    table = VMEM((NBD * SUB + PAD, LANES), jnp.float32)
    stage = VMEM((GRIDS * GRID_ROWS + PAD, LANES), jnp.float32)
    parts = pl.pallas_call(
        scatter,
        out_shape=(piece,) * 8,
        in_specs=[smem, hbm, hbm, hbm],
        out_specs=(vmem,) * 8,
        scratch_shapes=[
            table,
            stage,
            pltpu.SMEM((GRIDS, K), jnp.int32),
            pltpu.SMEM((GRIDS,), jnp.int32),
            pltpu.SemaphoreType.DMA((GRIDS,)),
            pltpu.SemaphoreType.DMA((2,)),
        ],
        compiler_params=params,
    )(where, *(pltpu.with_memory_space_constraint(v, pltpu.HBM) for v in (coef, block_ids, to_tiles(surplus))))
    parts = [own + send(other, OTHER_CORE) for other, own in zip(parts[:4], parts[4:])]
    got = [send(parts[k], own_line(k)) for k in (2, 1, 3)]
    share = parts[0] + got[0] + got[1] + got[2]
    got = [send(share, other_line(k)) for k in (3, 1, 2)]
    share = share + got[0] + got[1] + got[2]
    got = {k: send(share, own_line(k)) for k in (3, 1, 2)}
    line = [share, got[1], got[2], got[3]]
    across = [send(part, OTHER_CORE) for part in line]
    rows = (block_ids - base) * SUB
    out = pl.pallas_call(
        gather,
        out_shape=jax.ShapeDtypeStruct((GRIDS * GRID_ROWS, LANES), jnp.float32),
        in_specs=[smem, vmem] + [vmem] * 8,
        out_specs=hbm,
        scratch_shapes=[
            table,
            stage,
            pltpu.SMEM((GRIDS, K), jnp.int32),
            pltpu.SemaphoreType.DMA((GRIDS,)),
            pltpu.SemaphoreType.DMA,
        ],
        compiler_params=params,
    )(where, rows, *line, *across)
    return from_tiles(out, surplus.shape)


def solution(mesh):
    return jax.shard_map(
        local,
        mesh=mesh,
        in_specs=(P("grp", "dom", None), P("grp", "dom"), P("grp")),
        out_specs=P("grp", "dom", None),
        check_vma=False,
    )
```

```python
import jax
import jax.numpy as jnp
from jax import lax
from jax.experimental import pallas as pl
from jax.experimental.pallas import tpu as pltpu
from jax.sharding import PartitionSpec as P

GRIDS = 16
K = 128
BLK = 512
NBD = 1024
LANES = 128
SUB = BLK // LANES
GRID_ROWS = K * SUB
HALF = NBD // 2 * SUB
PIECE = HALF // 4
BATCH = 16
PAD = 64
VMEM = pltpu.VMEM
VMEM_LIMIT = 48 * 1024 * 1024


def device(x, y, core):
    return (x * 4 + y) * 2 + core


def pairs(partner):
    return [
        (device(x, y, c), device(*partner(x, y, c)))
        for x in range(4)
        for y in range(4)
        for c in range(2)
    ]


def far(line):
    if line == "x":
        return pairs(lambda x, y, c: (x ^ (3 - c), y, c))
    return pairs(lambda x, y, c: (x, y ^ (3 - c), c))


def along_y(step):
    return pairs(lambda x, y, c: (x, y ^ step, c))


NEAR_X = pairs(lambda x, y, c: (x ^ 1, y, c))
FAR_X = far("x")
OTHER_CORE = pairs(lambda x, y, c: (x, y, 1 - c))


def send(value, partner):
    return lax.ppermute(value, "grp", partner)


def to_tiles(value):
    g, slots, _ = value.shape
    return value.reshape(g, slots // 8, 8, SUB, LANES).transpose(0, 1, 3, 2, 4).reshape(-1, LANES)


def from_tiles(rows, shape):
    g, slots, blk = shape
    return rows.reshape(g, slots // 8, SUB, 8, LANES).transpose(0, 1, 3, 2, 4).reshape(shape)


def slot_rows(start, slot):
    return pl.ds(start + (slot // 8) * 8 * SUB + slot % 8, SUB, stride=8)


def block_rows(row):
    return pl.ds(pl.multiple_of(row, SUB), SUB)


def piece_rows(where_ref):
    x, core = where_ref[1], where_ref[2]
    rows = []
    for c in (core, 1 - core):
        for half, step in ((1 - c, 3 - c), (c, 3 - c), (c, 1), (c, 0)):
            rows.append(pl.ds(pl.multiple_of(half * HALF + (x ^ step) * PIECE, PIECE), PIECE))
    return rows


def scatter(where_ref, coef_hbm, ids_hbm, surplus_hbm, *refs):
    pieces, (table, stage, ids, coef, sems, small_sems) = refs[:8], refs[8:]

    def load(g):
        part = pl.ds(pl.multiple_of(g * GRID_ROWS, GRID_ROWS), GRID_ROWS)
        return pltpu.make_async_copy(surplus_hbm.at[part, :], stage.at[part, :], sems.at[g])

    ids_copy = pltpu.make_async_copy(ids_hbm, ids, small_sems.at[0])
    coef_copy = pltpu.make_async_copy(coef_hbm, coef, small_sems.at[1])
    ids_copy.start()
    coef_copy.start()
    for g in range(GRIDS):
        load(g).start()
    table[...] = jnp.zeros_like(table)
    base = where_ref[0]
    ids_copy.wait()
    coef_copy.wait()

    def add_grid(g, carry):
        load(g).wait()
        factor = coef[g].astype(jnp.float32)
        start = pl.multiple_of(g * GRID_ROWS, GRID_ROWS)
        for first in range(0, K, BATCH):
            slots = range(first, first + BATCH)
            rows = [block_rows((ids[g, j] - base) * SUB) for j in slots]
            sums = [table[r, :] + stage[slot_rows(start, j), :] * factor for r, j in zip(rows, slots)]
            for r, total in zip(rows, sums):
                table[r, :] = total
        return carry

    lax.fori_loop(0, GRIDS, add_grid, 0)
    for piece, rows in zip(pieces, piece_rows(where_ref)):
        piece[...] = table[rows, :]


def gather(where_ref, rows_vmem, *refs):
    pieces, (out_hbm, table, stage, rows_ref, sems, rows_sem) = refs[:8], refs[8:]
    rows_copy = pltpu.make_async_copy(rows_vmem, rows_ref, rows_sem)
    rows_copy.start()
    for piece, rows in zip(pieces, piece_rows(where_ref)):
        table[rows, :] = piece[...]
    rows_copy.wait()

    def store(g):
        part = pl.ds(pl.multiple_of(g * GRID_ROWS, GRID_ROWS), GRID_ROWS)
        return pltpu.make_async_copy(stage.at[part, :], out_hbm.at[part, :], sems.at[g])

    def copy_grid(g, carry):
        start = pl.multiple_of(g * GRID_ROWS, GRID_ROWS)
        for first in range(0, K, BATCH):
            slots = range(first, first + BATCH)
            values = [table[block_rows(rows_ref[g, j]), :] for j in slots]
            for j, value in zip(slots, values):
                stage[slot_rows(start, j), :] = value
        store(g).start()
        return carry

    lax.fori_loop(0, GRIDS, copy_grid, 0)
    for g in range(GRIDS):
        store(g).wait()


def local(surplus, block_ids, coef):
    index = lax.axis_index("grp")
    base = lax.axis_index("dom") * NBD
    where = jnp.stack([base, index >> 3, index & 1]).astype(jnp.int32)
    smem = pl.BlockSpec(memory_space=pltpu.SMEM)
    vmem = pl.BlockSpec(memory_space=VMEM)
    hbm = pl.BlockSpec(memory_space=pltpu.HBM)
    params = pltpu.CompilerParams(vmem_limit_bytes=VMEM_LIMIT)
    piece = jax.ShapeDtypeStruct((PIECE, LANES), jnp.float32)
    table = VMEM((NBD * SUB + PAD, LANES), jnp.float32)
    stage = VMEM((GRIDS * GRID_ROWS + PAD, LANES), jnp.float32)
    parts = pl.pallas_call(
        scatter,
        out_shape=(piece,) * 8,
        in_specs=[smem, hbm, hbm, hbm],
        out_specs=(vmem,) * 8,
        scratch_shapes=[
            table,
            stage,
            pltpu.SMEM((GRIDS, K), jnp.int32),
            pltpu.SMEM((GRIDS,), jnp.int32),
            pltpu.SemaphoreType.DMA((GRIDS,)),
            pltpu.SemaphoreType.DMA((2,)),
        ],
        compiler_params=params,
    )(where, *(pltpu.with_memory_space_constraint(v, pltpu.HBM) for v in (coef, block_ids, to_tiles(surplus))))
    swap = lambda value: send(value, OTHER_CORE)
    crossing, straight, near, own = [mine + swap(theirs) for mine, theirs in zip(parts[:4], parts[4:])]
    crossing = send(crossing, FAR_X)
    straight = send(straight, FAR_X)
    near = send(near, NEAR_X)
    share = own + straight + swap(crossing) + near
    got = [send(share, along_y(k)) for k in (3, 1, 2)]
    own = share + got[0] + got[1] + got[2]
    straight = send(own, FAR_X)
    other = swap(own)
    crossing = send(other, FAR_X)
    near = send(own, NEAR_X)
    mine = [swap(crossing), swap(straight), swap(near), other]
    rows = (block_ids - base) * SUB
    out = pl.pallas_call(
        gather,
        out_shape=jax.ShapeDtypeStruct((GRIDS * GRID_ROWS, LANES), jnp.float32),
        in_specs=[smem, vmem] + [vmem] * 8,
        out_specs=hbm,
        scratch_shapes=[
            table,
            stage,
            pltpu.SMEM((GRIDS, K), jnp.int32),
            pltpu.SemaphoreType.DMA((GRIDS,)),
            pltpu.SemaphoreType.DMA,
        ],
        compiler_params=params,
    )(where, rows, crossing, straight, near, own, *mine)
    return from_tiles(out, surplus.shape)


def solution(mesh):
    return jax.shard_map(
        local,
        mesh=mesh,
        in_specs=(P("grp", "dom", None), P("grp", "dom"), P("grp")),
        out_specs=P("grp", "dom", None),
        check_vma=False,
    )
```

```python
import jax
import jax.numpy as jnp
from jax import lax
from jax.experimental import pallas as pl
from jax.experimental.pallas import tpu as pltpu
from jax.sharding import PartitionSpec as P

GRIDS = 16
K = 128
BLK = 512
NBD = 1024
LANES = 128
SUB = BLK // LANES
GRID_ROWS = K * SUB
HALF = NBD // 2 * SUB
PIECE = HALF // 4
BATCH = 16
PAD = 64
VMEM = pltpu.VMEM
VMEM_LIMIT = 48 * 1024 * 1024


def device(x, y, core):
    return (x * 4 + y) * 2 + core


def pairs(partner):
    return [
        (device(x, y, c), device(*partner(x, y, c)))
        for x in range(4)
        for y in range(4)
        for c in range(2)
    ]


def along(axis_of, step_of):
    return pairs(
        lambda x, y, c: (x, y ^ step_of(c), c) if axis_of(c) else (x ^ step_of(c), y, c)
    )


CROSSING = along(lambda c: 1 - c, lambda c: 3 - c)
STRAIGHT = along(lambda c: c, lambda c: 3 - c)
NEAR = along(lambda c: c, lambda c: 1)
ACROSS = [along(lambda c: 1 - c, lambda c, step=step: step) for step in (3, 1, 2)]
OTHER_CORE = pairs(lambda x, y, c: (x, y, 1 - c))


def send(value, partner):
    return lax.ppermute(value, "grp", partner)


def to_tiles(value):
    g, slots, _ = value.shape
    return value.reshape(g, slots // 8, 8, SUB, LANES).transpose(0, 1, 3, 2, 4).reshape(-1, LANES)


def from_tiles(rows, shape):
    g, slots, blk = shape
    return rows.reshape(g, slots // 8, SUB, 8, LANES).transpose(0, 1, 3, 2, 4).reshape(shape)


def slot_rows(start, slot):
    return pl.ds(start + (slot // 8) * 8 * SUB + slot % 8, SUB, stride=8)


def block_rows(row):
    return pl.ds(pl.multiple_of(row, SUB), SUB)


def piece_rows(where_ref):
    core = where_ref[3]
    rows = []
    for c in (core, 1 - core):
        for half, step in ((1 - c, 3 - c), (c, 3 - c), (c, 1), (c, 0)):
            place = half * HALF + (where_ref[1 + half] ^ step) * PIECE
            rows.append(pl.ds(pl.multiple_of(place, PIECE), PIECE))
    return rows


def scatter(where_ref, coef_hbm, ids_hbm, surplus_hbm, *refs):
    pieces, (table, stage, ids, coef, sems, small_sems) = refs[:8], refs[8:]

    def load(g):
        part = pl.ds(pl.multiple_of(g * GRID_ROWS, GRID_ROWS), GRID_ROWS)
        return pltpu.make_async_copy(surplus_hbm.at[part, :], stage.at[part, :], sems.at[g])

    ids_copy = pltpu.make_async_copy(ids_hbm, ids, small_sems.at[0])
    coef_copy = pltpu.make_async_copy(coef_hbm, coef, small_sems.at[1])
    ids_copy.start()
    coef_copy.start()
    for g in range(GRIDS):
        load(g).start()
    table[...] = jnp.zeros_like(table)
    base = where_ref[0]
    ids_copy.wait()
    coef_copy.wait()

    def add_grid(g, carry):
        load(g).wait()
        factor = coef[g].astype(jnp.float32)
        start = pl.multiple_of(g * GRID_ROWS, GRID_ROWS)
        for first in range(0, K, BATCH):
            slots = range(first, first + BATCH)
            rows = [block_rows((ids[g, j] - base) * SUB) for j in slots]
            sums = [table[r, :] + stage[slot_rows(start, j), :] * factor for r, j in zip(rows, slots)]
            for r, total in zip(rows, sums):
                table[r, :] = total
        return carry

    lax.fori_loop(0, GRIDS, add_grid, 0)
    for piece, rows in zip(pieces, piece_rows(where_ref)):
        piece[...] = table[rows, :]


def gather(where_ref, rows_vmem, *refs):
    pieces, (out_hbm, table, stage, rows_ref, sems, rows_sem) = refs[:8], refs[8:]
    rows_copy = pltpu.make_async_copy(rows_vmem, rows_ref, rows_sem)
    rows_copy.start()
    for piece, rows in zip(pieces, piece_rows(where_ref)):
        table[rows, :] = piece[...]
    rows_copy.wait()

    def store(g):
        part = pl.ds(pl.multiple_of(g * GRID_ROWS, GRID_ROWS), GRID_ROWS)
        return pltpu.make_async_copy(stage.at[part, :], out_hbm.at[part, :], sems.at[g])

    def copy_grid(g, carry):
        start = pl.multiple_of(g * GRID_ROWS, GRID_ROWS)
        for first in range(0, K, BATCH):
            slots = range(first, first + BATCH)
            values = [table[block_rows(rows_ref[g, j]), :] for j in slots]
            for j, value in zip(slots, values):
                stage[slot_rows(start, j), :] = value
        store(g).start()
        return carry

    lax.fori_loop(0, GRIDS, copy_grid, 0)
    for g in range(GRIDS):
        store(g).wait()


def local(surplus, block_ids, coef):
    index = lax.axis_index("grp")
    base = lax.axis_index("dom") * NBD
    where = jnp.stack([base, index >> 3, (index >> 1) & 3, index & 1]).astype(jnp.int32)
    smem = pl.BlockSpec(memory_space=pltpu.SMEM)
    vmem = pl.BlockSpec(memory_space=VMEM)
    hbm = pl.BlockSpec(memory_space=pltpu.HBM)
    params = pltpu.CompilerParams(vmem_limit_bytes=VMEM_LIMIT)
    piece = jax.ShapeDtypeStruct((PIECE, LANES), jnp.float32)
    table = VMEM((NBD * SUB + PAD, LANES), jnp.float32)
    stage = VMEM((GRIDS * GRID_ROWS + PAD, LANES), jnp.float32)
    parts = pl.pallas_call(
        scatter,
        out_shape=(piece,) * 8,
        in_specs=[smem, hbm, hbm, hbm],
        out_specs=(vmem,) * 8,
        scratch_shapes=[
            table,
            stage,
            pltpu.SMEM((GRIDS, K), jnp.int32),
            pltpu.SMEM((GRIDS,), jnp.int32),
            pltpu.SemaphoreType.DMA((GRIDS,)),
            pltpu.SemaphoreType.DMA((2,)),
        ],
        compiler_params=params,
    )(where, *(pltpu.with_memory_space_constraint(v, pltpu.HBM) for v in (coef, block_ids, to_tiles(surplus))))
    swap = lambda value: send(value, OTHER_CORE)
    crossing, straight, near, own = [mine + swap(theirs) for mine, theirs in zip(parts[:4], parts[4:])]
    crossing = send(crossing, CROSSING)
    straight = send(straight, STRAIGHT)
    near = send(near, NEAR)
    share = own + straight + swap(crossing) + near
    got = [send(share, partner) for partner in ACROSS]
    own = share + got[0] + got[1] + got[2]
    straight = send(own, STRAIGHT)
    other = swap(own)
    crossing = send(other, CROSSING)
    near = send(own, NEAR)
    mine = [swap(crossing), swap(straight), swap(near), other]
    rows = (block_ids - base) * SUB
    out = pl.pallas_call(
        gather,
        out_shape=jax.ShapeDtypeStruct((GRIDS * GRID_ROWS, LANES), jnp.float32),
        in_specs=[smem, vmem] + [vmem] * 8,
        out_specs=hbm,
        scratch_shapes=[
            table,
            stage,
            pltpu.SMEM((GRIDS, K), jnp.int32),
            pltpu.SemaphoreType.DMA((GRIDS,)),
            pltpu.SemaphoreType.DMA,
        ],
        compiler_params=params,
    )(where, rows, crossing, straight, near, own, *mine)
    return from_tiles(out, surplus.shape)


def solution(mesh):
    return jax.shard_map(
        local,
        mesh=mesh,
        in_specs=(P("grp", "dom", None), P("grp", "dom"), P("grp")),
        out_specs=P("grp", "dom", None),
        check_vma=False,
    )
```

```python
import jax
import jax.numpy as jnp
from jax import lax
from jax.experimental import pallas as pl
from jax.experimental.pallas import tpu as pltpu
from jax.sharding import PartitionSpec as P

GRIDS = 16
K = 128
BLK = 512
NBD = 1024
LANES = 128
SUB = BLK // LANES
GRID_ROWS = K * SUB
HALF = NBD // 2 * SUB
PIECE = HALF // 4
ALL_BLOCKS = 8 * NBD
BATCH = 16
PAD = 64
ORDER = (0, 3, 1, 2)
VMEM = pltpu.VMEM
VMEM_LIMIT = 48 * 1024 * 1024


def device(x, y, core):
    return (x * 4 + y) * 2 + core


def pairs(partner):
    return [
        (device(x, y, c), device(*partner(x, y, c)))
        for x in range(4)
        for y in range(4)
        for c in range(2)
    ]


def own_line(step):
    return pairs(lambda x, y, c: (x, y ^ step, c) if c else (x ^ step, y, c))


def other_line(step):
    return pairs(lambda x, y, c: (x ^ step, y, c) if c else (x, y ^ step, c))


OTHER_CORE = pairs(lambda x, y, c: (x, y, 1 - c))


def send(value, partner):
    return lax.ppermute(value, "grp", partner)


def to_tiles(value):
    g, slots, _ = value.shape
    return value.reshape(g, slots // 8, 8, SUB, LANES).transpose(0, 1, 3, 2, 4).reshape(-1, LANES)


def from_tiles(rows, shape):
    g, slots, blk = shape
    return rows.reshape(g, slots // 8, SUB, 8, LANES).transpose(0, 1, 3, 2, 4).reshape(shape)


def slot_rows(start, slot):
    return pl.ds(start + (slot // 8) * 8 * SUB + slot % 8, SUB, stride=8)


def block_rows(row):
    return pl.ds(pl.multiple_of(row, SUB), SUB)


def piece_rows(where_ref, half, k, base=0):
    line = where_ref[1 + half]
    return pl.ds(pl.multiple_of(base + half * HALF + (line ^ k) * PIECE, PIECE), PIECE)


def scatter(where_ref, coef_hbm, ids_hbm, surplus_hbm, *refs):
    pieces, (table, stage, ids, coef, sems, small_sems) = refs[:8], refs[8:]

    def load(g):
        part = pl.ds(pl.multiple_of(g * GRID_ROWS, GRID_ROWS), GRID_ROWS)
        return pltpu.make_async_copy(surplus_hbm.at[part, :], stage.at[part, :], sems.at[g])

    ids_copy = pltpu.make_async_copy(ids_hbm, ids, small_sems.at[0])
    coef_copy = pltpu.make_async_copy(coef_hbm, coef, small_sems.at[1])
    ids_copy.start()
    coef_copy.start()
    for g in range(GRIDS):
        load(g).start()
    base = where_ref[0] * SUB
    own_rows = pl.ds(pl.multiple_of(base, NBD * SUB), NBD * SUB)
    table[own_rows, :] = jnp.zeros((NBD * SUB, LANES), jnp.float32)
    ids_copy.wait()
    coef_copy.wait()

    def add_grid(g, carry):
        load(g).wait()
        factor = coef[g].astype(jnp.float32)
        start = pl.multiple_of(g * GRID_ROWS, GRID_ROWS)
        for first in range(0, K, BATCH):
            slots = range(first, first + BATCH)
            rows = [block_rows(ids[g, j] * SUB) for j in slots]
            sums = [table[r, :] + stage[slot_rows(start, j), :] * factor for r, j in zip(rows, slots)]
            for r, total in zip(rows, sums):
                table[r, :] = total
        return carry

    lax.fori_loop(0, GRIDS, add_grid, 0)
    core = where_ref[3]
    for k in range(4):
        pieces[k][...] = table[piece_rows(where_ref, 1 - core, k, base), :]
        pieces[4 + k][...] = table[piece_rows(where_ref, core, k, base), :]


def gather(where_ref, rows_vmem, *refs):
    pieces, (out_hbm, table, stage, rows_ref, sems, rows_sem) = refs[:8], refs[8:]
    rows_copy = pltpu.make_async_copy(rows_vmem, rows_ref, rows_sem)
    rows_copy.start()
    core = where_ref[3]
    for i, k in enumerate(ORDER):
        table[piece_rows(where_ref, core, k), :] = pieces[i][...]
        table[piece_rows(where_ref, 1 - core, k), :] = pieces[4 + i][...]
    rows_copy.wait()

    def store(g):
        part = pl.ds(pl.multiple_of(g * GRID_ROWS, GRID_ROWS), GRID_ROWS)
        return pltpu.make_async_copy(stage.at[part, :], out_hbm.at[part, :], sems.at[g])

    def copy_grid(g, carry):
        start = pl.multiple_of(g * GRID_ROWS, GRID_ROWS)
        for first in range(0, K, BATCH):
            slots = range(first, first + BATCH)
            values = [table[block_rows(rows_ref[g, j]), :] for j in slots]
            for j, value in zip(slots, values):
                stage[slot_rows(start, j), :] = value
        store(g).start()
        return carry

    lax.fori_loop(0, GRIDS, copy_grid, 0)
    for g in range(GRIDS):
        store(g).wait()


def local(surplus, block_ids, coef):
    index = lax.axis_index("grp")
    base = lax.axis_index("dom") * NBD
    where = jnp.stack([base, index >> 3, (index >> 1) & 3, index & 1]).astype(jnp.int32)
    smem = pl.BlockSpec(memory_space=pltpu.SMEM)
    vmem = pl.BlockSpec(memory_space=VMEM)
    hbm = pl.BlockSpec(memory_space=pltpu.HBM)
    params = pltpu.CompilerParams(vmem_limit_bytes=VMEM_LIMIT)
    piece = jax.ShapeDtypeStruct((PIECE, LANES), jnp.float32)
    table = VMEM((NBD * SUB + PAD, LANES), jnp.float32)
    stage = VMEM((GRIDS * GRID_ROWS + PAD, LANES), jnp.float32)
    parts = pl.pallas_call(
        scatter,
        out_shape=(piece,) * 8,
        in_specs=[smem, hbm, hbm, hbm],
        out_specs=(vmem,) * 8,
        scratch_shapes=[
            VMEM((ALL_BLOCKS * SUB + PAD, LANES), jnp.float32),
            stage,
            pltpu.SMEM((GRIDS, K), jnp.int32),
            pltpu.SMEM((GRIDS,), jnp.int32),
            pltpu.SemaphoreType.DMA((GRIDS,)),
            pltpu.SemaphoreType.DMA((2,)),
        ],
        compiler_params=params,
    )(where, *(pltpu.with_memory_space_constraint(v, pltpu.HBM) for v in (coef, block_ids, to_tiles(surplus))))
    parts = [own + send(other, OTHER_CORE) for other, own in zip(parts[:4], parts[4:])]
    got = [send(parts[k], own_line(k)) for k in (2, 1, 3)]
    share = parts[0] + got[0] + got[1] + got[2]
    got = [send(share, other_line(k)) for k in (3, 1, 2)]
    share = share + got[0] + got[1] + got[2]
    line = [send(share, own_line(k)) if k else share for k in ORDER]
    across = [send(part, OTHER_CORE) for part in line]
    rows = (block_ids - base) * SUB
    out = pl.pallas_call(
        gather,
        out_shape=jax.ShapeDtypeStruct((GRIDS * GRID_ROWS, LANES), jnp.float32),
        in_specs=[smem, vmem] + [vmem] * 8,
        out_specs=hbm,
        scratch_shapes=[
            table,
            stage,
            pltpu.SMEM((GRIDS, K), jnp.int32),
            pltpu.SemaphoreType.DMA((GRIDS,)),
            pltpu.SemaphoreType.DMA,
        ],
        compiler_params=params,
    )(where, rows, *line, *across)
    return from_tiles(out, surplus.shape)


def solution(mesh):
    return jax.shard_map(
        local,
        mesh=mesh,
        in_specs=(P("grp", "dom", None), P("grp", "dom"), P("grp")),
        out_specs=P("grp", "dom", None),
        check_vma=False,
    )
```

```python
import jax
import jax.numpy as jnp
from jax import lax
from jax.experimental import pallas as pl
from jax.experimental.pallas import tpu as pltpu
from jax.sharding import PartitionSpec as P

GRIDS = 16
K = 128
BLK = 512
NBD = 1024
LANES = 128
SUB = BLK // LANES
GRID_ROWS = K * SUB
HALF = NBD // 2 * SUB
PIECE = HALF // 4
ALL_BLOCKS = 8 * NBD
BATCH = 16
PAD = 64
ORDER = (0, 3, 1, 2)
VMEM = pltpu.VMEM
VMEM_LIMIT = 48 * 1024 * 1024


def device(x, y, core):
    return (x * 4 + y) * 2 + core


def pairs(partner):
    return [
        (device(x, y, c), device(*partner(x, y, c)))
        for x in range(4)
        for y in range(4)
        for c in range(2)
    ]


def own_line(step):
    return pairs(lambda x, y, c: (x, y ^ step, c) if c else (x ^ step, y, c))


def other_line(step):
    return pairs(lambda x, y, c: (x ^ step, y, c) if c else (x, y ^ step, c))


OTHER_CORE = pairs(lambda x, y, c: (x, y, 1 - c))


def send(value, partner):
    return lax.ppermute(value, "grp", partner)


def to_tiles(value):
    g, slots, _ = value.shape
    return value.reshape(g, slots // 8, 8, SUB, LANES).transpose(0, 1, 3, 2, 4).reshape(-1, LANES)


def from_tiles(rows, shape):
    g, slots, blk = shape
    return rows.reshape(g, slots // 8, SUB, 8, LANES).transpose(0, 1, 3, 2, 4).reshape(shape)


def slot_rows(start, slot):
    return pl.ds(start + (slot // 8) * 8 * SUB + slot % 8, SUB, stride=8)


def block_rows(row):
    return pl.ds(pl.multiple_of(row, SUB), SUB)


def piece_rows(where_ref, half, k, base=0):
    line = where_ref[1 + half]
    return pl.ds(pl.multiple_of(base + half * HALF + (line ^ k) * PIECE, PIECE), PIECE)


def scatter(where_ref, coef_hbm, ids_hbm, surplus_hbm, *refs):
    pieces, (even, odd, stage, ids, coef, sems, small_sems) = refs[:8], refs[8:]

    def load(g):
        part = pl.ds(pl.multiple_of(g * GRID_ROWS, GRID_ROWS), GRID_ROWS)
        return pltpu.make_async_copy(surplus_hbm.at[part, :], stage.at[part, :], sems.at[g])

    ids_copy = pltpu.make_async_copy(ids_hbm, ids, small_sems.at[0])
    coef_copy = pltpu.make_async_copy(coef_hbm, coef, small_sems.at[1])
    ids_copy.start()
    coef_copy.start()
    for g in range(GRIDS):
        load(g).start()
    base = where_ref[0] * SUB
    own_rows = pl.ds(pl.multiple_of(base, NBD * SUB), NBD * SUB)
    for table in (even, odd):
        table[own_rows, :] = jnp.zeros((NBD * SUB, LANES), jnp.float32)
    ids_copy.wait()
    coef_copy.wait()

    def add_grid(g, carry):
        load(g).wait()
        factor = coef[g].astype(jnp.float32)
        start = pl.multiple_of(g * GRID_ROWS, GRID_ROWS)
        for first in range(0, K, BATCH):
            slots = range(first, first + BATCH)
            table = odd if first // BATCH % 2 else even
            rows = [block_rows(ids[g, j] * SUB) for j in slots]
            sums = [table[r, :] + stage[slot_rows(start, j), :] * factor for r, j in zip(rows, slots)]
            for r, total in zip(rows, sums):
                table[r, :] = total
        return carry

    lax.fori_loop(0, GRIDS, add_grid, 0)
    core = where_ref[3]
    for k in range(4):
        for piece, half in ((pieces[k], 1 - core), (pieces[4 + k], core)):
            rows = piece_rows(where_ref, half, k, base)
            piece[...] = even[rows, :] + odd[rows, :]


def gather(where_ref, rows_vmem, *refs):
    pieces, (out_hbm, table, stage, rows_ref, sems, rows_sem) = refs[:8], refs[8:]
    rows_copy = pltpu.make_async_copy(rows_vmem, rows_ref, rows_sem)
    rows_copy.start()
    core = where_ref[3]
    for i, k in enumerate(ORDER):
        table[piece_rows(where_ref, core, k), :] = pieces[i][...]
        table[piece_rows(where_ref, 1 - core, k), :] = pieces[4 + i][...]
    rows_copy.wait()

    def store(g):
        part = pl.ds(pl.multiple_of(g * GRID_ROWS, GRID_ROWS), GRID_ROWS)
        return pltpu.make_async_copy(stage.at[part, :], out_hbm.at[part, :], sems.at[g])

    def copy_grid(g, carry):
        start = pl.multiple_of(g * GRID_ROWS, GRID_ROWS)
        for first in range(0, K, BATCH):
            slots = range(first, first + BATCH)
            values = [table[block_rows(rows_ref[g, j]), :] for j in slots]
            for j, value in zip(slots, values):
                stage[slot_rows(start, j), :] = value
        store(g).start()
        return carry

    lax.fori_loop(0, GRIDS, copy_grid, 0)
    for g in range(GRIDS):
        store(g).wait()


def local(surplus, block_ids, coef):
    index = lax.axis_index("grp")
    base = lax.axis_index("dom") * NBD
    where = jnp.stack([base, index >> 3, (index >> 1) & 3, index & 1]).astype(jnp.int32)
    smem = pl.BlockSpec(memory_space=pltpu.SMEM)
    vmem = pl.BlockSpec(memory_space=VMEM)
    hbm = pl.BlockSpec(memory_space=pltpu.HBM)
    params = pltpu.CompilerParams(vmem_limit_bytes=VMEM_LIMIT)
    piece = jax.ShapeDtypeStruct((PIECE, LANES), jnp.float32)
    table = VMEM((NBD * SUB + PAD, LANES), jnp.float32)
    stage = VMEM((GRIDS * GRID_ROWS + PAD, LANES), jnp.float32)
    parts = pl.pallas_call(
        scatter,
        out_shape=(piece,) * 8,
        in_specs=[smem, hbm, hbm, hbm],
        out_specs=(vmem,) * 8,
        scratch_shapes=[
            VMEM((ALL_BLOCKS * SUB + PAD, LANES), jnp.float32),
            VMEM((ALL_BLOCKS * SUB + PAD, LANES), jnp.float32),
            stage,
            pltpu.SMEM((GRIDS, K), jnp.int32),
            pltpu.SMEM((GRIDS,), jnp.int32),
            pltpu.SemaphoreType.DMA((GRIDS,)),
            pltpu.SemaphoreType.DMA((2,)),
        ],
        compiler_params=params,
    )(where, *(pltpu.with_memory_space_constraint(v, pltpu.HBM) for v in (coef, block_ids, to_tiles(surplus))))
    parts = [own + send(other, OTHER_CORE) for other, own in zip(parts[:4], parts[4:])]
    got = [send(parts[k], own_line(k)) for k in (2, 1, 3)]
    share = parts[0] + got[0] + got[1] + got[2]
    got = [send(share, other_line(k)) for k in (3, 1, 2)]
    share = share + got[0] + got[1] + got[2]
    line = [send(share, own_line(k)) if k else share for k in ORDER]
    across = [send(part, OTHER_CORE) for part in line]
    rows = (block_ids - base) * SUB
    out = pl.pallas_call(
        gather,
        out_shape=jax.ShapeDtypeStruct((GRIDS * GRID_ROWS, LANES), jnp.float32),
        in_specs=[smem, vmem] + [vmem] * 8,
        out_specs=hbm,
        scratch_shapes=[
            table,
            stage,
            pltpu.SMEM((GRIDS, K), jnp.int32),
            pltpu.SemaphoreType.DMA((GRIDS,)),
            pltpu.SemaphoreType.DMA,
        ],
        compiler_params=params,
    )(where, rows, *line, *across)
    return from_tiles(out, surplus.shape)


def solution(mesh):
    return jax.shard_map(
        local,
        mesh=mesh,
        in_specs=(P("grp", "dom", None), P("grp", "dom"), P("grp")),
        out_specs=P("grp", "dom", None),
        check_vma=False,
    )
```

```python
import jax
import jax.numpy as jnp
from jax import lax
from jax.experimental import pallas as pl
from jax.experimental.pallas import tpu as pltpu
from jax.sharding import PartitionSpec as P

GRIDS = 16
K = 128
BLK = 512
NBD = 1024
LANES = 128
SUB = BLK // LANES
GRID_ROWS = K * SUB
HALF = NBD // 2 * SUB
PIECE = HALF // 4
ALL_BLOCKS = 8 * NBD
SCATTER_BATCH = 8
GATHER_BATCH = 16
PAD = 64
ORDER = (0, 3, 1, 2)
VMEM = pltpu.VMEM
VMEM_LIMIT = 48 * 1024 * 1024


def device(x, y, core):
    return (x * 4 + y) * 2 + core


def pairs(partner):
    return [
        (device(x, y, c), device(*partner(x, y, c)))
        for x in range(4)
        for y in range(4)
        for c in range(2)
    ]


def own_line(step):
    return pairs(lambda x, y, c: (x, y ^ step, c) if c else (x ^ step, y, c))


def other_line(step):
    return pairs(lambda x, y, c: (x ^ step, y, c) if c else (x, y ^ step, c))


OTHER_CORE = pairs(lambda x, y, c: (x, y, 1 - c))


def send(value, partner):
    return lax.ppermute(value, "grp", partner)


def to_tiles(value):
    g, slots, _ = value.shape
    return value.reshape(g, slots // 8, 8, SUB, LANES).transpose(0, 1, 3, 2, 4).reshape(-1, LANES)


def from_tiles(rows, shape):
    g, slots, blk = shape
    return rows.reshape(g, slots // 8, SUB, 8, LANES).transpose(0, 1, 3, 2, 4).reshape(shape)


def slot_rows(start, slot):
    return pl.ds(start + (slot // 8) * 8 * SUB + slot % 8, SUB, stride=8)


def block_rows(row):
    return pl.ds(pl.multiple_of(row, SUB), SUB)


def piece_rows(where_ref, half, k, base=0):
    line = where_ref[1 + half]
    return pl.ds(pl.multiple_of(base + half * HALF + (line ^ k) * PIECE, PIECE), PIECE)


def scatter(where_ref, coef_hbm, ids_hbm, surplus_hbm, *refs):
    pieces, (even, odd, stage, ids, coef, sems, small_sems) = refs[:8], refs[8:]

    def load(g):
        part = pl.ds(pl.multiple_of(g * GRID_ROWS, GRID_ROWS), GRID_ROWS)
        return pltpu.make_async_copy(surplus_hbm.at[part, :], stage.at[part, :], sems.at[g])

    ids_copy = pltpu.make_async_copy(ids_hbm, ids, small_sems.at[0])
    coef_copy = pltpu.make_async_copy(coef_hbm, coef, small_sems.at[1])
    ids_copy.start()
    coef_copy.start()
    for g in range(GRIDS):
        load(g).start()
    base = where_ref[0] * SUB
    own_rows = pl.ds(pl.multiple_of(base, NBD * SUB), NBD * SUB)
    for table in (even, odd):
        table[own_rows, :] = jnp.zeros((NBD * SUB, LANES), jnp.float32)
    ids_copy.wait()
    coef_copy.wait()

    def add_grid(g, carry):
        load(g).wait()
        factor = coef[g].astype(jnp.float32)
        start = pl.multiple_of(g * GRID_ROWS, GRID_ROWS)
        for first in range(0, K, SCATTER_BATCH):
            slots = range(first, first + SCATTER_BATCH)
            table = odd if first // SCATTER_BATCH % 2 else even
            rows = [block_rows(ids[g, j] * SUB) for j in slots]
            sums = [table[r, :] + stage[slot_rows(start, j), :] * factor for r, j in zip(rows, slots)]
            for r, total in zip(rows, sums):
                table[r, :] = total
        return carry

    lax.fori_loop(0, GRIDS, add_grid, 0)
    core = where_ref[3]
    for k in range(4):
        for piece, half in ((pieces[k], 1 - core), (pieces[4 + k], core)):
            rows = piece_rows(where_ref, half, k, base)
            piece[...] = even[rows, :] + odd[rows, :]


def gather(where_ref, rows_vmem, *refs):
    pieces, (out_hbm, table, stage, rows_ref, sems, rows_sem) = refs[:8], refs[8:]
    rows_copy = pltpu.make_async_copy(rows_vmem, rows_ref, rows_sem)
    rows_copy.start()
    core = where_ref[3]
    for i, k in enumerate(ORDER):
        table[piece_rows(where_ref, core, k), :] = pieces[i][...]
        table[piece_rows(where_ref, 1 - core, k), :] = pieces[4 + i][...]
    rows_copy.wait()

    stores = []
    for g in range(GRIDS):
        start = g * GRID_ROWS
        for first in range(0, K, GATHER_BATCH):
            slots = range(first, first + GATHER_BATCH)
            values = [table[block_rows(rows_ref[g, j]), :] for j in slots]
            for j, value in zip(slots, values):
                stage[slot_rows(start, j), :] = value
        part = pl.ds(start, GRID_ROWS)
        store = pltpu.make_async_copy(stage.at[part, :], out_hbm.at[part, :], sems.at[g])
        store.start()
        stores.append(store)
    for store in stores:
        store.wait()


def local(surplus, block_ids, coef):
    index = lax.axis_index("grp")
    base = lax.axis_index("dom") * NBD
    where = jnp.stack([base, index >> 3, (index >> 1) & 3, index & 1]).astype(jnp.int32)
    smem = pl.BlockSpec(memory_space=pltpu.SMEM)
    vmem = pl.BlockSpec(memory_space=VMEM)
    hbm = pl.BlockSpec(memory_space=pltpu.HBM)
    params = pltpu.CompilerParams(vmem_limit_bytes=VMEM_LIMIT)
    piece = jax.ShapeDtypeStruct((PIECE, LANES), jnp.float32)
    table = VMEM((NBD * SUB + PAD, LANES), jnp.float32)
    stage = VMEM((GRIDS * GRID_ROWS + PAD, LANES), jnp.float32)
    parts = pl.pallas_call(
        scatter,
        out_shape=(piece,) * 8,
        in_specs=[smem, hbm, hbm, hbm],
        out_specs=(vmem,) * 8,
        scratch_shapes=[
            VMEM((ALL_BLOCKS * SUB + PAD, LANES), jnp.float32),
            VMEM((ALL_BLOCKS * SUB + PAD, LANES), jnp.float32),
            stage,
            pltpu.SMEM((GRIDS, K), jnp.int32),
            pltpu.SMEM((GRIDS,), jnp.int32),
            pltpu.SemaphoreType.DMA((GRIDS,)),
            pltpu.SemaphoreType.DMA((2,)),
        ],
        compiler_params=params,
    )(where, *(pltpu.with_memory_space_constraint(v, pltpu.HBM) for v in (coef, block_ids, to_tiles(surplus))))
    parts = [own + send(other, OTHER_CORE) for other, own in zip(parts[:4], parts[4:])]
    got = [send(parts[k], own_line(k)) for k in (2, 1, 3)]
    share = parts[0] + got[0] + got[1] + got[2]
    got = [send(share, other_line(k)) for k in (3, 1, 2)]
    share = share + got[0] + got[1] + got[2]
    line = [send(share, own_line(k)) if k else share for k in ORDER]
    across = [send(part, OTHER_CORE) for part in line]
    rows = (block_ids - base) * SUB
    out = pl.pallas_call(
        gather,
        out_shape=jax.ShapeDtypeStruct((GRIDS * GRID_ROWS, LANES), jnp.float32),
        in_specs=[smem, vmem] + [vmem] * 8,
        out_specs=hbm,
        scratch_shapes=[
            table,
            stage,
            pltpu.SMEM((GRIDS, K), jnp.int32),
            pltpu.SemaphoreType.DMA((GRIDS,)),
            pltpu.SemaphoreType.DMA,
        ],
        compiler_params=params,
    )(where, rows, *line, *across)
    return from_tiles(out, surplus.shape)


def solution(mesh):
    return jax.shard_map(
        local,
        mesh=mesh,
        in_specs=(P("grp", "dom", None), P("grp", "dom"), P("grp")),
        out_specs=P("grp", "dom", None),
        check_vma=False,
    )
```

```python
import jax
import jax.numpy as jnp
from jax import lax
from jax.experimental import pallas as pl
from jax.experimental.pallas import tpu as pltpu
from jax.sharding import PartitionSpec as P

GRIDS = 16
K = 128
BLK = 512
NBD = 1024
LANES = 128
SUB = BLK // LANES
GRID_ROWS = K * SUB
HALF = NBD // 2 * SUB
PIECE = HALF // 4
ALL_BLOCKS = 8 * NBD
SCATTER_BATCH = 8
GATHER_BATCH = 16
PAD = 64
ORDER = (0, 3, 1, 2)
VMEM = pltpu.VMEM
VMEM_LIMIT = 48 * 1024 * 1024


def device(x, y, core):
    return (x * 4 + y) * 2 + core


def pairs(partner):
    return [
        (device(x, y, c), device(*partner(x, y, c)))
        for x in range(4)
        for y in range(4)
        for c in range(2)
    ]


def own_line(step):
    return pairs(lambda x, y, c: (x, y ^ step, c) if c else (x ^ step, y, c))


def other_line(step):
    return pairs(lambda x, y, c: (x ^ step, y, c) if c else (x, y ^ step, c))


OTHER_CORE = pairs(lambda x, y, c: (x, y, 1 - c))


def send(value, partner):
    return lax.ppermute(value, "grp", partner)


def to_tiles(value):
    g, slots, _ = value.shape
    return value.reshape(g, slots // 8, 8, SUB, LANES).transpose(0, 1, 3, 2, 4).reshape(-1, LANES)


def from_tiles(rows, shape):
    g, slots, blk = shape
    return rows.reshape(g, slots // 8, SUB, 8, LANES).transpose(0, 1, 3, 2, 4).reshape(shape)


def slot_rows(start, slot):
    return pl.ds(start + (slot // 8) * 8 * SUB + slot % 8, SUB, stride=8)


def block_rows(row):
    return pl.ds(pl.multiple_of(row, SUB), SUB)


def piece_rows(where_ref, half, k, base=0):
    line = where_ref[1 + half]
    return pl.ds(pl.multiple_of(base + half * HALF + (line ^ k) * PIECE, PIECE), PIECE)


def scatter(where_ref, coef_hbm, ids_hbm, surplus_hbm, *refs):
    pieces, (even, odd, stage, ids, coef, sems, small_sems) = refs[:8], refs[8:]

    def load(g):
        part = pl.ds(pl.multiple_of(g * GRID_ROWS, GRID_ROWS), GRID_ROWS)
        return pltpu.make_async_copy(surplus_hbm.at[part, :], stage.at[part, :], sems.at[g])

    ids_copy = pltpu.make_async_copy(ids_hbm, ids, small_sems.at[0])
    coef_copy = pltpu.make_async_copy(coef_hbm, coef, small_sems.at[1])
    ids_copy.start()
    coef_copy.start()
    for g in range(GRIDS):
        load(g).start()
    base = where_ref[0] * SUB
    own_rows = pl.ds(pl.multiple_of(base, NBD * SUB), NBD * SUB)
    for table in (even, odd):
        table[own_rows, :] = jnp.zeros((NBD * SUB, LANES), jnp.float32)
    ids_copy.wait()
    coef_copy.wait()

    def add_grid(g, carry):
        load(g).wait()
        factor = coef[g].astype(jnp.float32)
        start = pl.multiple_of(g * GRID_ROWS, GRID_ROWS)
        for first in range(0, K, SCATTER_BATCH):
            slots = range(first, first + SCATTER_BATCH)
            table = odd if first // SCATTER_BATCH % 2 else even
            rows = [block_rows(ids[g, j] * SUB) for j in slots]
            sums = [table[r, :] + stage[slot_rows(start, j), :] * factor for r, j in zip(rows, slots)]
            for r, total in zip(rows, sums):
                table[r, :] = total
        return carry

    lax.fori_loop(0, GRIDS, add_grid, 0)
    core = where_ref[3]
    for k in range(4):
        for piece, half in ((pieces[k], 1 - core), (pieces[4 + k], core)):
            rows = piece_rows(where_ref, half, k, base)
            piece[...] = even[rows, :] + odd[rows, :]


def gather(where_ref, rows_vmem, *refs):
    pieces, (out_hbm, table, stage, rows_ref, sems, rows_sem) = refs[:8], refs[8:]
    rows_copy = pltpu.make_async_copy(rows_vmem, rows_ref, rows_sem)
    rows_copy.start()
    core = where_ref[3]
    for i, k in enumerate(ORDER):
        table[piece_rows(where_ref, core, k), :] = pieces[i][...]
        table[piece_rows(where_ref, 1 - core, k), :] = pieces[4 + i][...]
    rows_copy.wait()

    stores = []
    for g in range(GRIDS):
        start = g * GRID_ROWS
        for first in range(0, K, GATHER_BATCH):
            slots = range(first, first + GATHER_BATCH)
            values = [table[block_rows(rows_ref[g, j]), :] for j in slots]
            for j, value in zip(slots, values):
                stage[slot_rows(start, j), :] = value
            done = (first + GATHER_BATCH) * SUB
            if done == GRID_ROWS or g == GRIDS - 1 and done == GRID_ROWS // 2:
                size = GRID_ROWS // 2 if g == GRIDS - 1 else GRID_ROWS
                part = pl.ds(start + done - size, size)
                copy = pltpu.make_async_copy(stage.at[part, :], out_hbm.at[part, :], sems.at[len(stores)])
                copy.start()
                stores.append(copy)
    for store in stores:
        store.wait()


def local(surplus, block_ids, coef):
    index = lax.axis_index("grp")
    base = lax.axis_index("dom") * NBD
    where = jnp.stack([base, index >> 3, (index >> 1) & 3, index & 1]).astype(jnp.int32)
    smem = pl.BlockSpec(memory_space=pltpu.SMEM)
    vmem = pl.BlockSpec(memory_space=VMEM)
    hbm = pl.BlockSpec(memory_space=pltpu.HBM)
    params = pltpu.CompilerParams(vmem_limit_bytes=VMEM_LIMIT)
    piece = jax.ShapeDtypeStruct((PIECE, LANES), jnp.float32)
    table = VMEM((NBD * SUB + PAD, LANES), jnp.float32)
    stage = VMEM((GRIDS * GRID_ROWS + PAD, LANES), jnp.float32)
    parts = pl.pallas_call(
        scatter,
        out_shape=(piece,) * 8,
        in_specs=[smem, hbm, hbm, hbm],
        out_specs=(vmem,) * 8,
        scratch_shapes=[
            VMEM((ALL_BLOCKS * SUB + PAD, LANES), jnp.float32),
            VMEM((ALL_BLOCKS * SUB + PAD, LANES), jnp.float32),
            stage,
            pltpu.SMEM((GRIDS, K), jnp.int32),
            pltpu.SMEM((GRIDS,), jnp.int32),
            pltpu.SemaphoreType.DMA((GRIDS,)),
            pltpu.SemaphoreType.DMA((2,)),
        ],
        compiler_params=params,
    )(where, *(pltpu.with_memory_space_constraint(v, pltpu.HBM) for v in (coef, block_ids, to_tiles(surplus))))
    parts = [own + send(other, OTHER_CORE) for other, own in zip(parts[:4], parts[4:])]
    got = [send(parts[k], own_line(k)) for k in (2, 1, 3)]
    share = parts[0] + got[0] + got[1] + got[2]
    got = [send(share, other_line(k)) for k in (3, 1, 2)]
    share = share + got[0] + got[1] + got[2]
    line = [send(share, own_line(k)) if k else share for k in ORDER]
    across = [send(part, OTHER_CORE) for part in line]
    rows = (block_ids - base) * SUB
    out = pl.pallas_call(
        gather,
        out_shape=jax.ShapeDtypeStruct((GRIDS * GRID_ROWS, LANES), jnp.float32),
        in_specs=[smem, vmem] + [vmem] * 8,
        out_specs=hbm,
        scratch_shapes=[
            table,
            stage,
            pltpu.SMEM((GRIDS, K), jnp.int32),
            pltpu.SemaphoreType.DMA((GRIDS + 1,)),
            pltpu.SemaphoreType.DMA,
        ],
        compiler_params=params,
    )(where, rows, *line, *across)
    return from_tiles(out, surplus.shape)


def solution(mesh):
    return jax.shard_map(
        local,
        mesh=mesh,
        in_specs=(P("grp", "dom", None), P("grp", "dom"), P("grp")),
        out_specs=P("grp", "dom", None),
        check_vma=False,
    )
```
